32 devices in a mesh: energy: 8 (over y, x, core), tile: 4 (over z).
Axes of the slice: x: 2, y: 2, z: 4, core: 2. Of those that a mesh axis runs over, the one named last changes fastest.
Arguments:
- lesser: float32 [2, 512, 4, 16384], P(None, 'energy', 'tile'), may hold values from -6 to 6
- greater: float32 [2, 512, 4, 16384], P(None, 'energy', 'tile'), may hold values from -6 to 6
Outputs:
- polarization: float32 [2, 512, 4, 16384], P(None, 'energy', 'tile')
The draws below stay inside these ranges and needn't reach their ends.
All inputs are finite; a program needn't handle non-finite values.
Results may differ from the reference program's by a relative error of at most 0.000098.
Values sent between devices are 32-bit elements; how exact they have to be, the bound alone decides.
No kernel may reach another device: no remote copies, remote signals or barrier semaphores. Data moves between devices by JAX's collectives and lax.ppermute only.
A program may use at most 192 MiB of HBM per device.

```python
import jax
import jax.numpy as jnp
from jax import lax

ENERGIES = 512
TILE_SIDE = 2
TILE_COUNT = 4
BLOCK_SIDE = 128
BLOCK_CELLS = 16384


def shard_levels(key, dims, cuts, smallest, largest):
    def one(dim, shards_of):
        heights = jax.random.uniform(jax.random.fold_in(jax.random.fold_in(key, 6), dim), (shards_of,), jnp.float32, smallest / len(cuts), largest / len(cuts))
        return jnp.repeat(jnp.exp(heights), dims[dim] // shards_of).reshape((-1,) + (1,) * (len(dims) - dim - 1))

    level = one(*cuts[0])
    for cut in cuts[1:]:
        level = level * one(*cut)
    return level


def gaussian(own_key, extent, scale, most, shards=(), held_as=jnp.bfloat16):
    entries = jax.random.normal(own_key, extent, jnp.float32) * scale
    if len(shards) > 0:
        entries = shard_levels(own_key, extent, shards, -0.22, 0.18) * entries
    return jnp.clip(entries, min=-most, max=most).astype(held_as)


def setup_inputs(seed: int = 0) -> dict:
    key_of = jax.random.split(jax.random.key(seed), 3)
    return {
        "lesser": gaussian(key_of[0], (2, ENERGIES, TILE_COUNT, BLOCK_CELLS), 1.0, 6.0, ((1, 8), (2, 4)), jnp.float32),
        "greater": gaussian(key_of[1], (2, ENERGIES, TILE_COUNT, BLOCK_CELLS), 1.0, 6.0, ((1, 8), (2, 4)), jnp.float32),
    }


def reference(lesser, greater):
    side = TILE_SIDE
    block = BLOCK_SIDE
    mirrored = greater.reshape(2, ENERGIES, side, side, block, block)
    mirrored = mirrored.transpose(0, 1, 3, 2, 5, 4).reshape(2, ENERGIES, TILE_COUNT, BLOCK_CELLS)
    length = 2 * ENERGIES

    def one_tile(pair):
        lesser_tile, greater_tile = pair
        lower = lesser_tile[0] + 1j * lesser_tile[1]
        upper = greater_tile[0] + 1j * greater_tile[1]
        front = jnp.fft.fft(lower, n=length, axis=0)
        other = jnp.fft.ifft(upper, n=length, axis=0) * length
        corr = jnp.fft.ifft(front * other, axis=0)[:ENERGIES]
        result = -1j * corr * (ENERGIES ** -0.5)
        return jnp.stack([jnp.real(result), jnp.imag(result)]).astype(lesser.dtype)

    outputs = lax.map(one_tile, (lesser.transpose(2, 0, 1, 3), mirrored.transpose(2, 0, 1, 3)))
    return outputs.transpose(1, 2, 0, 3)
```

```python
import functools
import math

import jax
import jax.numpy as jnp
import numpy as np
from jax import lax
from jax.experimental import pallas as pl
from jax.experimental.pallas import tpu as pltpu
from jax.sharding import PartitionSpec as P

LANES = 128
RADIX = 8
ANY = pl.BlockSpec(memory_space=pl.ANY)


def fit(extent, most):
    size = 1
    while size * 2 <= most and extent % (size * 2) == 0:
        size *= 2
    return size


def gather_kernel(count, spot_ref, *rest):
    for source, target in zip(rest[:count], rest[-count:], strict=True):
        planes, depth, lanes = source.shape
        flat = target.reshape(depth * planes, lanes)
        for plane in range(planes):
            flat[pl.ds(plane, depth, stride=planes), :] = source[plane]


def gather(field, spot, peers, hops, after):
    planes, rows, lanes = field.shape
    depth = rows // peers
    group = fit(planes, 32)
    count = len(hops)
    if depth % 8:
        field = field.reshape(planes, peers, depth, lanes)
        block = (group, None, depth, lanes)
        place = lambda hop: lambda step, spot: (step, spot[0] ^ hop, 0, 0)
    else:
        block = (group, depth, lanes)
        place = lambda hop: lambda step, spot: (step, spot[0] ^ hop, 0)
    return pl.pallas_call(
        functools.partial(gather_kernel, count),
        grid_spec=pltpu.PrefetchScalarGridSpec(
            num_scalar_prefetch=1,
            grid=(planes // group,),
            in_specs=[pl.BlockSpec(block, place(hop)) for hop in hops] + [ANY] * len(after),
            out_specs=[pl.BlockSpec((depth, group, lanes), lambda step, spot: (0, step, 0))]
            * count,
        ),
        out_shape=[jax.ShapeDtypeStruct((depth, planes, lanes), jnp.float32)] * count,
        name="gather",
    )(spot, *[field] * count, *after)


def pack_kernel(peers, chunks, flip, spot_ref, field_ref, *rest):
    outs, turned, sems = rest[-chunks - 2 : -2], rest[-2], rest[-1]
    step, steps = pl.program_id(0), pl.num_programs(0)
    planes, rows, lanes = field_ref.shape
    depth = rows // (peers * chunks)
    slot = step % 2

    def copies(at, slot):
        found = []
        cube = turned.at[slot].reshape(rows, planes, lanes)
        for chunk in range(chunks):
            for hop in range(peers):
                first = ((spot_ref[0] ^ hop) * chunks + chunk) * depth
                found.append(
                    pltpu.make_async_copy(
                        cube.at[pl.ds(first, depth)],
                        outs[chunk].at[hop, :, pl.ds(at * planes, planes), :],
                        sems.at[slot, len(found)],
                    )
                )
        return found

    @pl.when(step >= 2)
    def _():
        for copy in copies(step - 2, slot):
            copy.wait()

    flat = turned.at[slot]
    for plane in range(planes):
        value = field_ref[plane]
        if flip:
            value = value.T
        flat[pl.ds(plane, rows, stride=planes), :] = value
    for copy in copies(step, slot):
        copy.start()

    @pl.when(step == steps - 1)
    def _():
        for copy in copies(step, slot):
            copy.wait()

        @pl.when(steps > 1)
        def _():
            for copy in copies(step - 1, 1 - slot):
                copy.wait()


def pack(field, spot, peers, chunks, flip, after):
    planes, rows, lanes = field.shape
    depth = rows // (peers * chunks)
    group = fit(planes, 16)
    shape = jax.ShapeDtypeStruct((peers, depth, planes, lanes), jnp.float32)
    return pl.pallas_call(
        functools.partial(pack_kernel, peers, chunks, flip),
        grid_spec=pltpu.PrefetchScalarGridSpec(
            num_scalar_prefetch=1,
            grid=(planes // group,),
            in_specs=[pl.BlockSpec((group, rows, lanes), lambda step, spot: (step, 0, 0))]
            + [ANY] * len(after),
            out_specs=[ANY] * chunks,
            scratch_shapes=[
                pltpu.VMEM((2, rows * group, lanes), jnp.float32),
                pltpu.SemaphoreType.DMA((2, peers * chunks)),
            ],
        ),
        out_shape=[shape] * chunks,
        name="pack",
    )(spot, field, *after)


def fan_kernel(count, apart_ref, near, far, *rest):
    outs, (held, came, left) = rest[-count - 3 : -3], rest[-3:]

    def arrivals(source):
        return [pltpu.make_async_copy(source.at[i], held.at[i], came.at[i]) for i in range(count)]

    apart = apart_ref[0] != 0

    @pl.when(apart)
    def _():
        for copy in arrivals(far):
            copy.start()

    @pl.when(jnp.logical_not(apart))
    def _():
        for copy in arrivals(near):
            copy.start()

    copies = [pltpu.make_async_copy(held.at[i], outs[i], left.at[i]) for i in range(count)]
    for arrival, copy in zip(arrivals(far), copies, strict=True):
        arrival.wait()
        copy.start()
    for copy in copies:
        copy.wait()


def fan(near, far, apart, after):
    count = near.shape[0]
    return pl.pallas_call(
        functools.partial(fan_kernel, count),
        grid_spec=pltpu.PrefetchScalarGridSpec(
            num_scalar_prefetch=1,
            grid=(1,),
            in_specs=[ANY] * (2 + len(after)),
            out_specs=[ANY] * count,
            scratch_shapes=[
                pltpu.VMEM(near.shape, near.dtype),
                pltpu.SemaphoreType.DMA((count,)),
                pltpu.SemaphoreType.DMA((count,)),
            ],
        ),
        out_shape=[jax.ShapeDtypeStruct(near.shape[1:], near.dtype)] * count,
        name="fan",
    )(apart, near, far, *after)


def unpack_kernel(peers, chunks, spot_ref, *rest):
    pieces = rest[: peers * chunks]
    out_ref, turned, sems = rest[-3:]
    step, steps = pl.program_id(0), pl.num_programs(0)
    planes, lead, _, rows, lanes = out_ref.shape
    depth = lead * rows // (peers * chunks)

    def copies(at, slot):
        found = []
        cube = turned.at[slot].reshape(lead * rows, planes, lanes)
        for chunk in range(chunks):
            for hop in range(peers):
                first = ((spot_ref[0] ^ hop) * chunks + chunk) * depth
                found.append(
                    pltpu.make_async_copy(
                        pieces[chunk * peers + hop].at[:, pl.ds(at * planes, planes), :],
                        cube.at[pl.ds(first, depth)],
                        sems.at[slot, len(found)],
                    )
                )
        return found

    slot = step % 2

    @pl.when(step == 0)
    def _():
        for copy in copies(step, slot):
            copy.start()

    @pl.when(step + 1 < steps)
    def _():
        for copy in copies(step + 1, 1 - slot):
            copy.start()

    for copy in copies(step, slot):
        copy.wait()
    flat = turned.at[slot]
    for plane in range(planes):
        value = flat[pl.ds(plane, lead * rows, stride=planes), :]
        out_ref[plane, :, 0] = value.reshape(lead, rows, lanes)


def unpack(groups, part, parts, spot, before):
    chunks, peers = len(groups), len(groups[0])
    flat = [piece for group in groups for piece in group]
    depth, planes, lanes = flat[0].shape
    lead = peers if parts > 1 else 1
    rows = depth * peers * chunks // lead
    group = fit(planes, 16)
    return pl.pallas_call(
        functools.partial(unpack_kernel, peers, chunks),
        grid_spec=pltpu.PrefetchScalarGridSpec(
            num_scalar_prefetch=1,
            grid=(planes // group,),
            in_specs=[ANY] * (peers * chunks + len(before)),
            out_specs=pl.BlockSpec(
                (group, lead, 1, rows, lanes), lambda step, spot: (step, 0, part, 0, 0)
            ),
            scratch_shapes=[
                pltpu.VMEM((2, lead * rows * group, lanes), jnp.float32),
                pltpu.SemaphoreType.DMA((2, peers * chunks)),
            ],
        ),
        input_output_aliases={1 + len(flat): 0} if before else {},
        out_shape=jax.ShapeDtypeStruct((planes, lead, parts, rows, lanes), jnp.float32),
        name="unpack",
    )(spot, *flat, *before)


def split(value):
    high = value.astype(jnp.bfloat16)
    return high, (value - high.astype(jnp.float32)).astype(jnp.bfloat16)


def quarter(a, b, c, d, sign):
    s0 = (a[0] + c[0], a[1] + c[1])
    s1 = (a[0] - c[0], a[1] - c[1])
    t0 = (b[0] + d[0], b[1] + d[1])
    u = (b[0] - d[0], b[1] - d[1])
    t1 = (u[1], -u[0]) if sign < 0 else (-u[1], u[0])
    return (
        (s0[0] + t0[0], s0[1] + t0[1]),
        (s1[0] + t1[0], s1[1] + t1[1]),
        (s0[0] - t0[0], s0[1] - t0[1]),
        (s1[0] - t1[0], s1[1] - t1[1]),
    )


def correlate_kernel(peers, chunk, spot_ref, cos_ref, sin_ref, fore_ref, back_ref, *rest):
    lesser, greater = rest[:peers], rest[peers : 2 * peers]
    outs = rest[2 * peers : 3 * peers]
    sources, high, low, partial, result, sems = rest[3 * peers :]
    depth, _, energies, lanes = result.shape
    local = energies // peers
    base = energies // 4
    half = math.sqrt(0.5)
    slab = 16

    copies = []
    for kind, pieces in enumerate((lesser, greater)):
        for hop in range(peers):
            first = pl.multiple_of((spot_ref[0] ^ hop) * local, local)
            source = pieces[hop].at[pl.ds(chunk * depth, depth)] if kind == 0 else pieces[hop]
            copies.append(
                pltpu.make_async_copy(
                    source,
                    sources.at[kind, :, :, pl.ds(first, local), :],
                    sems.at[len(copies)],
                )
            )
            copies[-1].start()
    for copy in copies:
        copy.wait()

    for kind in range(2):
        for row in range(depth):
            columns = pl.ds((kind * depth + row) * lanes, lanes)

            def fold(step, carry, kind=kind, row=row, columns=columns):
                at = pl.multiple_of(step * slab, slab)
                x = []
                for q in range(4):
                    real = sources[kind, row, 0, pl.ds(q * base + at, slab), :]
                    imag = sources[kind, row, 1, pl.ds(q * base + at, slab), :]
                    x.append((real, imag if kind == 0 else -imag))
                even = quarter(x[0], x[1], x[2], x[3], -1)
                b, c, d = x[1], x[2], x[3]
                b = (half * (b[0] + b[1]), half * (b[1] - b[0]))
                c = (c[1], -c[0])
                d = (half * (d[1] - d[0]), -half * (d[0] + d[1]))
                odd = quarter(x[0], b, c, d, -1)
                for r in range(RADIX):
                    real, imag = (odd if r % 2 else even)[r // 2]
                    if r:
                        cosine = cos_ref[r, pl.ds(at, slab), :]
                        sine = sin_ref[r, pl.ds(at, slab), :]
                        real, imag = real * cosine + imag * sine, imag * cosine - real * sine
                    for part, value in enumerate((real, imag)):
                        upper, lower = split(value)
                        high[r, pl.ds(part * base + at, slab), columns] = upper
                        low[r, pl.ds(part * base + at, slab), columns] = lower
                return carry

            lax.fori_loop(0, base // slab, fold, 0)

    def product(matrix, upper, lower):
        dot = functools.partial(jnp.dot, preferred_element_type=jnp.float32)
        return dot(matrix[0], upper) + (dot(matrix[0], lower) + dot(matrix[1], upper))

    width = depth * lanes

    def multiply(r, carry):
        spectrum = product(fore_ref, high[r], low[r])
        ar, ai = spectrum[:base, :width], spectrum[base:, :width]
        br, bi = spectrum[:base, width:], spectrum[base:, width:]
        merged = jnp.concatenate([ar * br + ai * bi, ai * br - ar * bi], axis=0)
        upper, lower = split(merged)
        partial[r] = product(back_ref, upper, lower)
        return carry

    lax.fori_loop(0, RADIX, multiply, 0)

    for row in range(depth):
        columns = pl.ds(row * lanes, lanes)

        def unfold(step, carry, row=row, columns=columns):
            at = pl.multiple_of(step * slab, slab)
            z = []
            for r in range(RADIX):
                real = partial[r, pl.ds(at, slab), columns]
                imag = partial[r, pl.ds(base + at, slab), columns]
                if r:
                    cosine = cos_ref[r, pl.ds(at, slab), :]
                    sine = sin_ref[r, pl.ds(at, slab), :]
                    real, imag = real * cosine - imag * sine, imag * cosine + real * sine
                z.append((real, imag))
            even = quarter(z[0], z[2], z[4], z[6], 1)
            odd = quarter(z[1], z[3], z[5], z[7], 1)
            turned = (
                odd[0],
                (half * (odd[1][0] - odd[1][1]), half * (odd[1][0] + odd[1][1])),
                (-odd[2][1], odd[2][0]),
                (-half * (odd[3][0] + odd[3][1]), half * (odd[3][0] - odd[3][1])),
            )
            for q in range(4):
                real = even[q][0] + turned[q][0]
                imag = even[q][1] + turned[q][1]
                result[row, 0, pl.ds(q * base + at, slab), :] = imag
                result[row, 1, pl.ds(q * base + at, slab), :] = -real
            return carry

        lax.fori_loop(0, base // slab, unfold, 0)

    copies = []
    for hop in range(peers):
        first = pl.multiple_of((spot_ref[0] ^ hop) * local, local)
        copies.append(
            pltpu.make_async_copy(
                result.at[:, :, pl.ds(first, local), :], outs[hop], sems.at[hop]
            )
        )
        copies[-1].start()
    for copy in copies:
        copy.wait()


def tables(energies):
    base = energies // 4
    length = RADIX * base
    turn = np.outer(np.arange(RADIX), np.arange(base)) * (2.0 * np.pi / length)
    phase = np.outer(np.arange(base), np.arange(base)) % base * (2.0 * np.pi / base)
    cosine, sine = np.cos(phase), np.sin(phase)
    fore = np.block([[cosine, sine], [-sine, cosine]])
    back = fore.T / (length * math.sqrt(energies))

    def two(matrix):
        matrix = matrix.astype(np.float32)
        upper = matrix.astype(jnp.bfloat16)
        lower = (matrix - upper.astype(np.float32)).astype(jnp.bfloat16)
        return np.stack([upper, lower])

    return np.cos(turn).astype(np.float32), np.sin(turn).astype(np.float32), two(fore), two(back)


def correlate(lesser, greater, chunk, spot, cosine, sine, fore, back, energies):
    peers = len(lesser)
    depth, planes, lanes = greater[1].shape
    base = energies // 4
    local = planes // 2
    width = depth * lanes
    pieces = [
        piece.reshape(piece.shape[:-2] + (2, local, lanes)) for piece in (*lesser, *greater)
    ]
    shape = jax.ShapeDtypeStruct((depth, 2, local, lanes), jnp.float32)
    whole = lambda value: pl.BlockSpec(value.shape, lambda step, spot: (0,) * value.ndim)
    found = pl.pallas_call(
        functools.partial(correlate_kernel, peers, chunk),
        grid_spec=pltpu.PrefetchScalarGridSpec(
            num_scalar_prefetch=1,
            grid=(1,),
            in_specs=[whole(cosine), whole(sine), whole(fore), whole(back)] + [ANY] * (2 * peers),
            out_specs=[ANY] * peers,
            scratch_shapes=[
                pltpu.VMEM((2, depth, 2, energies, lanes), jnp.float32),
                pltpu.VMEM((RADIX, 2 * base, 2 * width), jnp.bfloat16),
                pltpu.VMEM((RADIX, 2 * base, 2 * width), jnp.bfloat16),
                pltpu.VMEM((RADIX, 2 * base, width), jnp.float32),
                pltpu.VMEM((depth, 2, energies, lanes), jnp.float32),
                pltpu.SemaphoreType.DMA((2 * peers,)),
            ],
        ),
        out_shape=[shape] * peers,
        name="correlate",
    )(spot, cosine, sine, fore, back, *pieces)
    return [piece.reshape(depth, planes, lanes) for piece in found]


def exchange(pieces):
    peers = len(pieces)
    moved = [pieces[0]]
    for hop in range(1, peers):
        pairs = [(source, source ^ hop) for source in range(peers)]
        moved.append(lax.ppermute(pieces[hop], "energy", pairs))
    return moved


def mirrored_tile(tile, side):
    return tile % side * side + tile // side


def mirror(field):
    tiles = lax.axis_size("tile")
    side = math.isqrt(tiles)
    pairs = [(tile, mirrored_tile(tile, side)) for tile in range(tiles)]
    return lax.ppermute(field, "tile", [pair for pair in pairs if pair[0] != pair[1]])


def on_device(lesser, greater):
    peers = lax.axis_size("energy")
    local, cells = greater.shape[1], greater.shape[3]
    energies = local * peers
    block = math.isqrt(cells)
    planes, rows = 2 * local, cells // LANES
    chunks = fit(rows // peers, 4)
    spot = lax.axis_index("energy").astype(jnp.int32)[None]

    tile, side = lax.axis_index("tile"), math.isqrt(lax.axis_size("tile"))
    apart = (mirrored_tile(tile, side) != tile).astype(jnp.int32)[None]

    flip = block == LANES
    if not flip:
        greater = greater.reshape(planes, block, block).swapaxes(1, 2)
    greater = greater.reshape(planes, rows, LANES)
    lesser = lesser.reshape(planes, rows, LANES)
    order = sorted(range(peers), key=lambda hop: (-(hop.bit_count()), hop))
    early, late = order[: peers // 2], order[peers // 2 :]
    first = gather(lesser, spot, peers, early, [])
    greater_out = pack(greater, spot, peers, chunks, flip, first[:1])
    second = gather(lesser, spot, peers, late, greater_out[:1])
    lesser_out = [None] * peers
    for hop, piece in zip(early + late, [*first, *second], strict=True):
        lesser_out[hop] = piece

    cosine, sine, fore, back = tables(energies)
    wide = (RADIX, energies // 4, LANES)
    cosine = jnp.broadcast_to(cosine[:, :, None], wide)
    sine = jnp.broadcast_to(sine[:, :, None], wide)
    fore, back = jnp.asarray(fore), jnp.asarray(back)

    lesser_in = exchange(lesser_out)
    mirrored = [mirror(field) for field in greater_out]
    found, polars = [], []
    parts = 2 if chunks % 2 == 0 and rows // peers % 16 == 0 else 1
    each = chunks // parts
    result = []
    for chunk in range(chunks):
        pieces = fan(
            greater_out[chunk], mirrored[chunk], apart, [polar[0] for polar in polars[-2:-1]]
        )
        greater_in = exchange(pieces)
        polar = correlate(
            lesser_in, greater_in, chunk, spot, cosine, sine, fore, back, energies
        )
        polars.append(polar)
        found.append(exchange(polar))
        if (chunk + 1) % each == 0:
            result = [unpack(found[-each:], chunk // each, parts, spot, result)]
    return result[0].reshape(2, local, 1, cells)


def solution(mesh):
    return jax.shard_map(
        on_device,
        mesh=mesh,
        in_specs=(P(None, "energy", "tile", None), P(None, "energy", "tile", None)),
        out_specs=P(None, "energy", "tile", None),
        check_vma=False,
    )
```

```python
import functools
import math

import jax
import jax.numpy as jnp
import numpy as np
from jax import lax
from jax.experimental import pallas as pl
from jax.experimental.pallas import tpu as pltpu
from jax.sharding import PartitionSpec as P


LANES = 128
RADIX = 8
ANY = pl.BlockSpec(memory_space=pl.ANY)


def fit(extent, most):
    size = 1
    while size * 2 <= most and extent % (size * 2) == 0:
        size *= 2
    return size


def turn(source, target):
    outer, inner, lanes = source.shape
    if outer % 8 == 0 and inner % 8 == 0:
        for i in range(0, outer, 8):
            for j in range(0, inner, 8):
                value = jnp.swapaxes(source[i : i + 8, j : j + 8, :], 0, 1)
                target[j : j + 8, i : i + 8, :] = value
    else:
        flat = target.reshape(inner * outer, lanes)
        for i in range(outer):
            flat[pl.ds(i, inner, stride=outer), :] = source[i]


def gather_kernel(count, spot_ref, *rest):
    for source, target in zip(rest[:count], rest[-count:], strict=True):
        turn(source, target)


def gather(field, spot, peers, hops, after):
    planes, rows, lanes = field.shape
    depth = rows // peers
    group = fit(planes, 64)
    count = len(hops)
    if depth % 8:
        field = field.reshape(planes, peers, depth, lanes)
        block = (group, None, depth, lanes)
        place = lambda hop: lambda step, spot: (step, spot[0] ^ hop, 0, 0)
    else:
        block = (group, depth, lanes)
        place = lambda hop: lambda step, spot: (step, spot[0] ^ hop, 0)
    return pl.pallas_call(
        functools.partial(gather_kernel, count),
        grid_spec=pltpu.PrefetchScalarGridSpec(
            num_scalar_prefetch=1,
            grid=(planes // group,),
            in_specs=[pl.BlockSpec(block, place(hop)) for hop in hops] + [ANY] * len(after),
            out_specs=[pl.BlockSpec((depth, group, lanes), lambda step, spot: (0, step, 0))]
            * count,
        ),
        out_shape=[jax.ShapeDtypeStruct((depth, planes, lanes), jnp.float32)] * count,
        name="gather",
    )(spot, *[field] * count, *after)


def pack_kernel(peers, chunks, flip, spot_ref, field_ref, *rest):
    outs, turned, sems = rest[-chunks - 2 : -2], rest[-2], rest[-1]
    step, steps = pl.program_id(0), pl.num_programs(0)
    planes, rows, lanes = field_ref.shape
    depth = rows // (peers * chunks)
    slot = step % 2

    def copies(at, slot):
        found = []
        cube = turned.at[slot].reshape(rows, planes, lanes)
        for chunk in range(chunks):
            for hop in range(peers):
                first = ((spot_ref[0] ^ hop) * chunks + chunk) * depth
                found.append(
                    pltpu.make_async_copy(
                        cube.at[pl.ds(first, depth)],
                        outs[chunk].at[hop, :, pl.ds(at * planes, planes), :],
                        sems.at[slot, len(found)],
                    )
                )
        return found

    @pl.when(step >= 2)
    def _():
        for copy in copies(step - 2, slot):
            copy.wait()

    cube = turned.at[slot].reshape(rows, planes, lanes)
    if flip:
        for plane in range(0, planes, 8):
            value = jnp.transpose(field_ref[plane : plane + 8], (2, 0, 1))
            cube[:, plane : plane + 8, :] = value
    else:
        turn(field_ref, cube)
    for copy in copies(step, slot):
        copy.start()

    @pl.when(step == steps - 1)
    def _():
        for copy in copies(step, slot):
            copy.wait()

        @pl.when(steps > 1)
        def _():
            for copy in copies(step - 1, 1 - slot):
                copy.wait()


def pack(field, spot, peers, chunks, flip, after):
    planes, rows, lanes = field.shape
    depth = rows // (peers * chunks)
    group = fit(planes, 32)
    shape = jax.ShapeDtypeStruct((peers, depth, planes, lanes), jnp.float32)
    return pl.pallas_call(
        functools.partial(pack_kernel, peers, chunks, flip),
        grid_spec=pltpu.PrefetchScalarGridSpec(
            num_scalar_prefetch=1,
            grid=(planes // group,),
            in_specs=[pl.BlockSpec((group, rows, lanes), lambda step, spot: (step, 0, 0))]
            + [ANY] * len(after),
            out_specs=[ANY] * chunks,
            scratch_shapes=[
                pltpu.VMEM((2, rows * group, lanes), jnp.float32),
                pltpu.SemaphoreType.DMA((2, peers * chunks)),
            ],
        ),
        out_shape=[shape] * chunks,
        name="pack",
    )(spot, field, *after)


def fan_kernel(count, apart_ref, near, far, *rest):
    outs, (held, came, left) = rest[-count - 3 : -3], rest[-3:]

    def arrivals(source):
        return [pltpu.make_async_copy(source.at[i], held.at[i], came.at[i]) for i in range(count)]

    apart = apart_ref[0] != 0

    @pl.when(apart)
    def _():
        for copy in arrivals(far):
            copy.start()

    @pl.when(jnp.logical_not(apart))
    def _():
        for copy in arrivals(near):
            copy.start()

    copies = [pltpu.make_async_copy(held.at[i], outs[i], left.at[i]) for i in range(count)]
    for arrival, copy in zip(arrivals(far), copies, strict=True):
        arrival.wait()
        copy.start()
    for copy in copies:
        copy.wait()


def fan(near, far, apart, after):
    count = near.shape[0]
    return pl.pallas_call(
        functools.partial(fan_kernel, count),
        grid_spec=pltpu.PrefetchScalarGridSpec(
            num_scalar_prefetch=1,
            grid=(1,),
            in_specs=[ANY] * (2 + len(after)),
            out_specs=[ANY] * count,
            scratch_shapes=[
                pltpu.VMEM(near.shape, near.dtype),
                pltpu.SemaphoreType.DMA((count,)),
                pltpu.SemaphoreType.DMA((count,)),
            ],
        ),
        out_shape=[jax.ShapeDtypeStruct(near.shape[1:], near.dtype)] * count,
        name="fan",
    )(apart, near, far, *after)


def unpack_kernel(peers, chunks, spot_ref, *rest):
    pieces = rest[: peers * chunks]
    out_ref, turned, sems = rest[-3:]
    step, steps = pl.program_id(0), pl.num_programs(0)
    planes, lead, _, rows, lanes = out_ref.shape
    depth = lead * rows // (peers * chunks)

    def copies(at, slot):
        found = []
        cube = turned.at[slot].reshape(lead * rows, planes, lanes)
        for chunk in range(chunks):
            for hop in range(peers):
                first = ((spot_ref[0] ^ hop) * chunks + chunk) * depth
                found.append(
                    pltpu.make_async_copy(
                        pieces[chunk * peers + hop].at[:, pl.ds(at * planes, planes), :],
                        cube.at[pl.ds(first, depth)],
                        sems.at[slot, len(found)],
                    )
                )
        return found

    slot = step % 2

    @pl.when(step == 0)
    def _():
        for copy in copies(step, slot):
            copy.start()

    @pl.when(step + 1 < steps)
    def _():
        for copy in copies(step + 1, 1 - slot):
            copy.start()

    for copy in copies(step, slot):
        copy.wait()
    cube = turned.at[slot].reshape(lead, rows, planes, lanes)
    for i in range(lead):
        turn(cube.at[i], out_ref.at[:, i, 0])


def unpack(groups, part, parts, spot, before):
    chunks, peers = len(groups), len(groups[0])
    flat = [piece for group in groups for piece in group]
    depth, planes, lanes = flat[0].shape
    lead = peers if parts > 1 else 1
    rows = depth * peers * chunks // lead
    group = fit(planes, 64)
    return pl.pallas_call(
        functools.partial(unpack_kernel, peers, chunks),
        grid_spec=pltpu.PrefetchScalarGridSpec(
            num_scalar_prefetch=1,
            grid=(planes // group,),
            in_specs=[ANY] * (peers * chunks + len(before)),
            out_specs=pl.BlockSpec(
                (group, lead, 1, rows, lanes), lambda step, spot: (step, 0, part, 0, 0)
            ),
            scratch_shapes=[
                pltpu.VMEM((2, lead * rows * group, lanes), jnp.float32),
                pltpu.SemaphoreType.DMA((2, peers * chunks)),
            ],
        ),
        input_output_aliases={1 + len(flat): 0} if before else {},
        out_shape=jax.ShapeDtypeStruct((planes, lead, parts, rows, lanes), jnp.float32),
        name="unpack",
    )(spot, *flat, *before)


def split(value):
    high = value.astype(jnp.bfloat16)
    return high, (value - high.astype(jnp.float32)).astype(jnp.bfloat16)


def quarter(a, b, c, d, sign):
    s0 = (a[0] + c[0], a[1] + c[1])
    s1 = (a[0] - c[0], a[1] - c[1])
    t0 = (b[0] + d[0], b[1] + d[1])
    u = (b[0] - d[0], b[1] - d[1])
    t1 = (u[1], -u[0]) if sign < 0 else (-u[1], u[0])
    return (
        (s0[0] + t0[0], s0[1] + t0[1]),
        (s1[0] + t1[0], s1[1] + t1[1]),
        (s0[0] - t0[0], s0[1] - t0[1]),
        (s1[0] - t1[0], s1[1] - t1[1]),
    )


def correlate_kernel(peers, chunk, spot_ref, cos_ref, sin_ref, fore_ref, back_ref, *rest):
    lesser, greater = rest[:peers], rest[peers : 2 * peers]
    outs = rest[2 * peers : 3 * peers]
    sources, high, low, partial, result, sems = rest[3 * peers :]
    depth, _, energies, lanes = result.shape
    local = energies // peers
    base = energies // 4
    half = math.sqrt(0.5)
    slab = 16

    copies = []
    for kind, pieces in enumerate((lesser, greater)):
        for hop in range(peers):
            first = pl.multiple_of((spot_ref[0] ^ hop) * local, local)
            source = pieces[hop].at[pl.ds(chunk * depth, depth)] if kind == 0 else pieces[hop]
            copies.append(
                pltpu.make_async_copy(
                    source,
                    sources.at[kind, :, :, pl.ds(first, local), :],
                    sems.at[len(copies)],
                )
            )
            copies[-1].start()
    for copy in copies:
        copy.wait()

    for kind in range(2):
        for row in range(depth):
            columns = pl.ds((kind * depth + row) * lanes, lanes)

            def fold(step, carry, kind=kind, row=row, columns=columns):
                at = pl.multiple_of(step * slab, slab)
                x = []
                for q in range(4):
                    real = sources[kind, row, 0, pl.ds(q * base + at, slab), :]
                    imag = sources[kind, row, 1, pl.ds(q * base + at, slab), :]
                    x.append((real, imag if kind == 0 else -imag))
                even = quarter(x[0], x[1], x[2], x[3], -1)
                b, c, d = x[1], x[2], x[3]
                b = (half * (b[0] + b[1]), half * (b[1] - b[0]))
                c = (c[1], -c[0])
                d = (half * (d[1] - d[0]), -half * (d[0] + d[1]))
                odd = quarter(x[0], b, c, d, -1)
                for r in range(RADIX):
                    real, imag = (odd if r % 2 else even)[r // 2]
                    if r:
                        cosine = cos_ref[r, pl.ds(at, slab), :]
                        sine = sin_ref[r, pl.ds(at, slab), :]
                        real, imag = real * cosine + imag * sine, imag * cosine - real * sine
                    for part, value in enumerate((real, imag)):
                        upper, lower = split(value)
                        high[r, pl.ds(part * base + at, slab), columns] = upper
                        low[r, pl.ds(part * base + at, slab), columns] = lower
                return carry

            lax.fori_loop(0, base // slab, fold, 0)

    def product(matrix, upper, lower):
        dot = functools.partial(jnp.dot, preferred_element_type=jnp.float32)
        return dot(matrix[0], upper) + (dot(matrix[0], lower) + dot(matrix[1], upper))

    width = depth * lanes

    def multiply(r, carry):
        spectrum = product(fore_ref, high[r], low[r])
        ar, ai = spectrum[:base, :width], spectrum[base:, :width]
        br, bi = spectrum[:base, width:], spectrum[base:, width:]
        merged = jnp.concatenate([ar * br + ai * bi, ai * br - ar * bi], axis=0)
        upper, lower = split(merged)
        partial[r] = product(back_ref, upper, lower)
        return carry

    lax.fori_loop(0, RADIX, multiply, 0)

    for row in range(depth):
        columns = pl.ds(row * lanes, lanes)

        def unfold(step, carry, row=row, columns=columns):
            at = pl.multiple_of(step * slab, slab)
            z = []
            for r in range(RADIX):
                real = partial[r, pl.ds(at, slab), columns]
                imag = partial[r, pl.ds(base + at, slab), columns]
                if r:
                    cosine = cos_ref[r, pl.ds(at, slab), :]
                    sine = sin_ref[r, pl.ds(at, slab), :]
                    real, imag = real * cosine - imag * sine, imag * cosine + real * sine
                z.append((real, imag))
            even = quarter(z[0], z[2], z[4], z[6], 1)
            odd = quarter(z[1], z[3], z[5], z[7], 1)
            turned = (
                odd[0],
                (half * (odd[1][0] - odd[1][1]), half * (odd[1][0] + odd[1][1])),
                (-odd[2][1], odd[2][0]),
                (-half * (odd[3][0] + odd[3][1]), half * (odd[3][0] - odd[3][1])),
            )
            for q in range(4):
                real = even[q][0] + turned[q][0]
                imag = even[q][1] + turned[q][1]
                result[row, 0, pl.ds(q * base + at, slab), :] = imag
                result[row, 1, pl.ds(q * base + at, slab), :] = -real
            return carry

        lax.fori_loop(0, base // slab, unfold, 0)

    copies = []
    for hop in range(peers):
        first = pl.multiple_of((spot_ref[0] ^ hop) * local, local)
        copies.append(
            pltpu.make_async_copy(
                result.at[:, :, pl.ds(first, local), :], outs[hop], sems.at[hop]
            )
        )
        copies[-1].start()
    for copy in copies:
        copy.wait()


def tables(energies):
    base = energies // 4
    length = RADIX * base
    turn = np.outer(np.arange(RADIX), np.arange(base)) * (2.0 * np.pi / length)
    phase = np.outer(np.arange(base), np.arange(base)) % base * (2.0 * np.pi / base)
    cosine, sine = np.cos(phase), np.sin(phase)
    fore = np.block([[cosine, sine], [-sine, cosine]])
    back = fore.T / (length * math.sqrt(energies))

    def two(matrix):
        matrix = matrix.astype(np.float32)
        upper = matrix.astype(jnp.bfloat16)
        lower = (matrix - upper.astype(np.float32)).astype(jnp.bfloat16)
        return np.stack([upper, lower])

    return np.cos(turn).astype(np.float32), np.sin(turn).astype(np.float32), two(fore), two(back)


def correlate(lesser, greater, chunk, spot, cosine, sine, fore, back, energies):
    peers = len(lesser)
    depth, planes, lanes = greater[1].shape
    base = energies // 4
    local = planes // 2
    width = depth * lanes
    pieces = [
        piece.reshape(piece.shape[:-2] + (2, local, lanes)) for piece in (*lesser, *greater)
    ]
    shape = jax.ShapeDtypeStruct((depth, 2, local, lanes), jnp.float32)
    whole = lambda value: pl.BlockSpec(value.shape, lambda step, spot: (0,) * value.ndim)
    found = pl.pallas_call(
        functools.partial(correlate_kernel, peers, chunk),
        grid_spec=pltpu.PrefetchScalarGridSpec(
            num_scalar_prefetch=1,
            grid=(1,),
            in_specs=[whole(cosine), whole(sine), whole(fore), whole(back)] + [ANY] * (2 * peers),
            out_specs=[ANY] * peers,
            scratch_shapes=[
                pltpu.VMEM((2, depth, 2, energies, lanes), jnp.float32),
                pltpu.VMEM((RADIX, 2 * base, 2 * width), jnp.bfloat16),
                pltpu.VMEM((RADIX, 2 * base, 2 * width), jnp.bfloat16),
                pltpu.VMEM((RADIX, 2 * base, width), jnp.float32),
                pltpu.VMEM((depth, 2, energies, lanes), jnp.float32),
                pltpu.SemaphoreType.DMA((2 * peers,)),
            ],
        ),
        out_shape=[shape] * peers,
        name="correlate",
    )(spot, cosine, sine, fore, back, *pieces)
    return [piece.reshape(depth, planes, lanes) for piece in found]


def swapped(piece, hop):
    if hop == 0:
        return piece
    pairs = [(source, source ^ hop) for source in range(lax.axis_size("energy"))]
    return lax.ppermute(piece, "energy", pairs)


def exchange(pieces):
    return [swapped(piece, hop) for hop, piece in enumerate(pieces)]


def mirrored_tile(tile, side):
    return tile % side * side + tile // side


def mirror(field):
    tiles = lax.axis_size("tile")
    side = math.isqrt(tiles)
    pairs = [(tile, mirrored_tile(tile, side)) for tile in range(tiles)]
    return lax.ppermute(field, "tile", [pair for pair in pairs if pair[0] != pair[1]])


def on_device(lesser, greater):
    peers = lax.axis_size("energy")
    local, cells = greater.shape[1], greater.shape[3]
    energies = local * peers
    block = math.isqrt(cells)
    planes, rows = 2 * local, cells // LANES
    chunks = fit(rows // peers, 4)
    spot = lax.axis_index("energy").astype(jnp.int32)[None]

    tile, side = lax.axis_index("tile"), math.isqrt(lax.axis_size("tile"))
    apart = (mirrored_tile(tile, side) != tile).astype(jnp.int32)[None]

    flip = block == LANES
    if not flip:
        greater = greater.reshape(planes, block, block).swapaxes(1, 2)
    greater = greater.reshape(planes, rows, LANES)
    lesser = lesser.reshape(planes, rows, LANES)
    hops = sorted(range(peers), key=lambda hop: (-(hop.bit_count()), hop))
    early, late = hops[: peers // 2], hops[peers // 2 :]
    lesser_in = [None] * peers
    first = gather(lesser, spot, peers, early, [])
    for hop, piece in zip(early, first, strict=True):
        lesser_in[hop] = swapped(piece, hop)
    greater_out = pack(greater, spot, peers, chunks, flip, first[:1])
    second = gather(lesser, spot, peers, late, greater_out[:1])
    for hop, piece in zip(late, second, strict=True):
        lesser_in[hop] = swapped(piece, hop)

    cosine, sine, fore, back = tables(energies)
    wide = (RADIX, energies // 4, LANES)
    cosine = jnp.broadcast_to(cosine[:, :, None], wide)
    sine = jnp.broadcast_to(sine[:, :, None], wide)
    fore, back = jnp.asarray(fore), jnp.asarray(back)

    mirrored = [mirror(field) for field in greater_out]
    found, polars = [], []
    parts = 2 if chunks % 2 == 0 and rows // peers % 16 == 0 else 1
    each = chunks // parts
    result = []
    for chunk in range(chunks):
        pieces = fan(
            greater_out[chunk], mirrored[chunk], apart, [polar[0] for polar in polars[-2:-1]]
        )
        greater_in = exchange(pieces)
        polar = correlate(
            lesser_in, greater_in, chunk, spot, cosine, sine, fore, back, energies
        )
        polars.append(polar)
        found.append(exchange(polar))
        if (chunk + 1) % each == 0:
            result = [unpack(found[-each:], chunk // each, parts, spot, result)]
    return result[0].reshape(2, local, 1, cells)


def solution(mesh):
    return jax.shard_map(
        on_device,
        mesh=mesh,
        in_specs=(P(None, "energy", "tile", None), P(None, "energy", "tile", None)),
        out_specs=P(None, "energy", "tile", None),
        check_vma=False,
    )
```

```python
import functools
import math

import jax
import jax.numpy as jnp
import numpy as np
from jax import lax
from jax.experimental import pallas as pl
from jax.experimental.pallas import tpu as pltpu
from jax.sharding import PartitionSpec as P


LANES = 128
RADIX = 8
ANY = pl.BlockSpec(memory_space=pl.ANY)


def fit(extent, most):
    size = 1
    while size * 2 <= most and extent % (size * 2) == 0:
        size *= 2
    return size


def turn(source, target):
    outer, inner, lanes = source.shape
    if outer % 8 == 0 and inner % 8 == 0:
        for i in range(0, outer, 8):
            for j in range(0, inner, 8):
                value = jnp.swapaxes(source[i : i + 8, j : j + 8, :], 0, 1)
                target[j : j + 8, i : i + 8, :] = value
    else:
        flat = target.reshape(inner * outer, lanes)
        for i in range(outer):
            flat[pl.ds(i, inner, stride=outer), :] = source[i]


def gather_kernel(count, spot_ref, *rest):
    for source, target in zip(rest[:count], rest[-count:], strict=True):
        turn(source, target)


def gather(field, spot, peers, hops, after):
    planes, rows, lanes = field.shape
    depth = rows // peers
    group = fit(planes, 64)
    count = len(hops)
    if depth % 8:
        field = field.reshape(planes, peers, depth, lanes)
        block = (group, None, depth, lanes)
        place = lambda hop: lambda step, spot: (step, spot[0] ^ hop, 0, 0)
    else:
        block = (group, depth, lanes)
        place = lambda hop: lambda step, spot: (step, spot[0] ^ hop, 0)
    return pl.pallas_call(
        functools.partial(gather_kernel, count),
        grid_spec=pltpu.PrefetchScalarGridSpec(
            num_scalar_prefetch=1,
            grid=(planes // group,),
            in_specs=[pl.BlockSpec(block, place(hop)) for hop in hops] + [ANY] * len(after),
            out_specs=[pl.BlockSpec((depth, group, lanes), lambda step, spot: (0, step, 0))]
            * count,
        ),
        out_shape=[jax.ShapeDtypeStruct((depth, planes, lanes), jnp.float32)] * count,
        name="gather",
    )(spot, *[field] * count, *after)


def pack_kernel(peers, chunks, flip, spot_ref, field_ref, *rest):
    outs, turned, sems = rest[-chunks - 2 : -2], rest[-2], rest[-1]
    step, steps = pl.program_id(0), pl.num_programs(0)
    planes, rows, lanes = field_ref.shape
    depth = rows // (peers * chunks)
    slot = step % 2

    def copies(at, slot):
        found = []
        cube = turned.at[slot].reshape(rows, planes, lanes)
        for chunk in range(chunks):
            for hop in range(peers):
                first = ((spot_ref[0] ^ hop) * chunks + chunk) * depth
                found.append(
                    pltpu.make_async_copy(
                        cube.at[pl.ds(first, depth)],
                        outs[chunk].at[hop, :, pl.ds(at * planes, planes), :],
                        sems.at[slot, len(found)],
                    )
                )
        return found

    @pl.when(step >= 2)
    def _():
        for copy in copies(step - 2, slot):
            copy.wait()

    cube = turned.at[slot].reshape(rows, planes, lanes)
    if flip:
        for plane in range(0, planes, 8):
            value = jnp.transpose(field_ref[plane : plane + 8], (2, 0, 1))
            cube[:, plane : plane + 8, :] = value
    else:
        turn(field_ref, cube)
    for copy in copies(step, slot):
        copy.start()

    @pl.when(step == steps - 1)
    def _():
        for copy in copies(step, slot):
            copy.wait()

        @pl.when(steps > 1)
        def _():
            for copy in copies(step - 1, 1 - slot):
                copy.wait()


def pack(field, spot, peers, chunks, flip, after):
    planes, rows, lanes = field.shape
    depth = rows // (peers * chunks)
    group = fit(planes, 32)
    shape = jax.ShapeDtypeStruct((peers, depth, planes, lanes), jnp.float32)
    return pl.pallas_call(
        functools.partial(pack_kernel, peers, chunks, flip),
        grid_spec=pltpu.PrefetchScalarGridSpec(
            num_scalar_prefetch=1,
            grid=(planes // group,),
            in_specs=[pl.BlockSpec((group, rows, lanes), lambda step, spot: (step, 0, 0))]
            + [ANY] * len(after),
            out_specs=[ANY] * chunks,
            scratch_shapes=[
                pltpu.VMEM((2, rows * group, lanes), jnp.float32),
                pltpu.SemaphoreType.DMA((2, peers * chunks)),
            ],
        ),
        out_shape=[shape] * chunks,
        name="pack",
    )(spot, field, *after)


def fan_kernel(count, apart_ref, near, far, *rest):
    outs, (held, came, left) = rest[-count - 3 : -3], rest[-3:]

    def arrivals(source):
        return [pltpu.make_async_copy(source.at[i], held.at[i], came.at[i]) for i in range(count)]

    apart = apart_ref[0] != 0

    @pl.when(apart)
    def _():
        for copy in arrivals(far):
            copy.start()

    @pl.when(jnp.logical_not(apart))
    def _():
        for copy in arrivals(near):
            copy.start()

    copies = [pltpu.make_async_copy(held.at[i], outs[i], left.at[i]) for i in range(count)]
    for arrival, copy in zip(arrivals(far), copies, strict=True):
        arrival.wait()
        copy.start()
    for copy in copies:
        copy.wait()


def fan(near, far, apart, after):
    count = near.shape[0]
    return pl.pallas_call(
        functools.partial(fan_kernel, count),
        grid_spec=pltpu.PrefetchScalarGridSpec(
            num_scalar_prefetch=1,
            grid=(1,),
            in_specs=[ANY] * (2 + len(after)),
            out_specs=[ANY] * count,
            scratch_shapes=[
                pltpu.VMEM(near.shape, near.dtype),
                pltpu.SemaphoreType.DMA((count,)),
                pltpu.SemaphoreType.DMA((count,)),
            ],
        ),
        out_shape=[jax.ShapeDtypeStruct(near.shape[1:], near.dtype)] * count,
        name="fan",
    )(apart, near, far, *after)


def unpack_kernel(peers, chunks, spot_ref, *rest):
    pieces = rest[: peers * chunks]
    out_ref, turned, sems = rest[-3:]
    step, steps = pl.program_id(0), pl.num_programs(0)
    planes, lead, _, rows, lanes = out_ref.shape
    depth = lead * rows // (peers * chunks)

    def copies(at, slot):
        found = []
        cube = turned.at[slot].reshape(lead * rows, planes, lanes)
        for chunk in range(chunks):
            for hop in range(peers):
                first = ((spot_ref[0] ^ hop) * chunks + chunk) * depth
                found.append(
                    pltpu.make_async_copy(
                        pieces[chunk * peers + hop].at[:, pl.ds(at * planes, planes), :],
                        cube.at[pl.ds(first, depth)],
                        sems.at[slot, len(found)],
                    )
                )
        return found

    slot = step % 2

    @pl.when(step == 0)
    def _():
        for copy in copies(step, slot):
            copy.start()

    @pl.when(step + 1 < steps)
    def _():
        for copy in copies(step + 1, 1 - slot):
            copy.start()

    for copy in copies(step, slot):
        copy.wait()
    cube = turned.at[slot].reshape(lead, rows, planes, lanes)
    for i in range(lead):
        turn(cube.at[i], out_ref.at[:, i, 0])


def unpack(groups, part, parts, spot, before):
    chunks, peers = len(groups), len(groups[0])
    flat = [piece for group in groups for piece in group]
    depth, planes, lanes = flat[0].shape
    lead = peers if parts > 1 else 1
    rows = depth * peers * chunks // lead
    group = fit(planes, 64)
    return pl.pallas_call(
        functools.partial(unpack_kernel, peers, chunks),
        grid_spec=pltpu.PrefetchScalarGridSpec(
            num_scalar_prefetch=1,
            grid=(planes // group,),
            in_specs=[ANY] * (peers * chunks + len(before)),
            out_specs=pl.BlockSpec(
                (group, lead, 1, rows, lanes), lambda step, spot: (step, 0, part, 0, 0)
            ),
            scratch_shapes=[
                pltpu.VMEM((2, lead * rows * group, lanes), jnp.float32),
                pltpu.SemaphoreType.DMA((2, peers * chunks)),
            ],
        ),
        input_output_aliases={1 + len(flat): 0} if before else {},
        out_shape=jax.ShapeDtypeStruct((planes, lead, parts, rows, lanes), jnp.float32),
        name="unpack",
    )(spot, *flat, *before)


def split(value):
    high = value.astype(jnp.bfloat16)
    return high, (value - high.astype(jnp.float32)).astype(jnp.bfloat16)


def quarter(a, b, c, d, sign):
    s0 = (a[0] + c[0], a[1] + c[1])
    s1 = (a[0] - c[0], a[1] - c[1])
    t0 = (b[0] + d[0], b[1] + d[1])
    u = (b[0] - d[0], b[1] - d[1])
    t1 = (u[1], -u[0]) if sign < 0 else (-u[1], u[0])
    return (
        (s0[0] + t0[0], s0[1] + t0[1]),
        (s1[0] + t1[0], s1[1] + t1[1]),
        (s0[0] - t0[0], s0[1] - t0[1]),
        (s1[0] - t1[0], s1[1] - t1[1]),
    )


def correlate_kernel(peers, chunk, spot_ref, cos_ref, sin_ref, fore_ref, back_ref, *rest):
    lesser, greater = rest[:peers], rest[peers : 2 * peers]
    outs = rest[2 * peers : 3 * peers]
    sources, high, low, partial, result, came, left = rest[3 * peers :]
    depth, _, energies, lanes = result.shape
    local = energies // peers
    base = energies // 4
    half = math.sqrt(0.5)
    slab = 16

    arrivals = ([], [])
    for kind, pieces in enumerate((lesser, greater)):
        for hop in range(peers):
            first = pl.multiple_of((spot_ref[0] ^ hop) * local, local)
            source = pieces[hop].at[pl.ds(chunk * depth, depth)] if kind == 0 else pieces[hop]
            copy = pltpu.make_async_copy(
                source, sources.at[kind, :, :, pl.ds(first, local), :], came.at[kind, hop]
            )
            copy.start()
            arrivals[kind].append(copy)

    for kind in range(2):
        for copy in arrivals[kind]:
            copy.wait()
        for row in range(depth):
            columns = pl.ds((kind * depth + row) * lanes, lanes)

            def fold(step, carry, kind=kind, row=row, columns=columns):
                at = pl.multiple_of(step * slab, slab)
                x = []
                for q in range(4):
                    real = sources[kind, row, 0, pl.ds(q * base + at, slab), :]
                    imag = sources[kind, row, 1, pl.ds(q * base + at, slab), :]
                    x.append((real, imag if kind == 0 else -imag))
                even = quarter(x[0], x[1], x[2], x[3], -1)
                b, c, d = x[1], x[2], x[3]
                b = (half * (b[0] + b[1]), half * (b[1] - b[0]))
                c = (c[1], -c[0])
                d = (half * (d[1] - d[0]), -half * (d[0] + d[1]))
                odd = quarter(x[0], b, c, d, -1)
                for r in range(RADIX):
                    real, imag = (odd if r % 2 else even)[r // 2]
                    if r:
                        cosine = cos_ref[r, pl.ds(at, slab), :]
                        sine = sin_ref[r, pl.ds(at, slab), :]
                        real, imag = real * cosine + imag * sine, imag * cosine - real * sine
                    for part, value in enumerate((real, imag)):
                        upper, lower = split(value)
                        high[r, pl.ds(part * base + at, slab), columns] = upper
                        low[r, pl.ds(part * base + at, slab), columns] = lower
                return carry

            lax.fori_loop(0, base // slab, fold, 0)

    def product(matrix, upper, lower):
        dot = functools.partial(jnp.dot, preferred_element_type=jnp.float32)
        return dot(matrix[0], upper) + (dot(matrix[0], lower) + dot(matrix[1], upper))

    width = depth * lanes

    def multiply(r, carry):
        spectrum = product(fore_ref, high[r], low[r])
        ar, ai = spectrum[:base, :width], spectrum[base:, :width]
        br, bi = spectrum[:base, width:], spectrum[base:, width:]
        merged = jnp.concatenate([ar * br + ai * bi, ai * br - ar * bi], axis=0)
        upper, lower = split(merged)
        partial[r] = product(back_ref, upper, lower)
        return carry

    lax.fori_loop(0, RADIX, multiply, 0, unroll=4)

    departures = []
    for row in range(depth):
        columns = pl.ds(row * lanes, lanes)

        def unfold(step, carry, row=row, columns=columns):
            at = pl.multiple_of(step * slab, slab)
            z = []
            for r in range(RADIX):
                real = partial[r, pl.ds(at, slab), columns]
                imag = partial[r, pl.ds(base + at, slab), columns]
                if r:
                    cosine = cos_ref[r, pl.ds(at, slab), :]
                    sine = sin_ref[r, pl.ds(at, slab), :]
                    real, imag = real * cosine - imag * sine, imag * cosine + real * sine
                z.append((real, imag))
            even = quarter(z[0], z[2], z[4], z[6], 1)
            odd = quarter(z[1], z[3], z[5], z[7], 1)
            turned = (
                odd[0],
                (half * (odd[1][0] - odd[1][1]), half * (odd[1][0] + odd[1][1])),
                (-odd[2][1], odd[2][0]),
                (-half * (odd[3][0] + odd[3][1]), half * (odd[3][0] - odd[3][1])),
            )
            for q in range(4):
                real = even[q][0] + turned[q][0]
                imag = even[q][1] + turned[q][1]
                result[row, 0, pl.ds(q * base + at, slab), :] = imag
                result[row, 1, pl.ds(q * base + at, slab), :] = -real
            return carry

        lax.fori_loop(0, base // slab, unfold, 0)
        for hop in range(peers):
            first = pl.multiple_of((spot_ref[0] ^ hop) * local, local)
            copy = pltpu.make_async_copy(
                result.at[row, :, pl.ds(first, local), :], outs[hop].at[row], left.at[row, hop]
            )
            copy.start()
            departures.append(copy)
    for copy in departures:
        copy.wait()


def tables(energies):
    base = energies // 4
    length = RADIX * base
    turn = np.outer(np.arange(RADIX), np.arange(base)) * (2.0 * np.pi / length)
    phase = np.outer(np.arange(base), np.arange(base)) % base * (2.0 * np.pi / base)
    cosine, sine = np.cos(phase), np.sin(phase)
    fore = np.block([[cosine, sine], [-sine, cosine]])
    back = fore.T / (length * math.sqrt(energies))

    def two(matrix):
        matrix = matrix.astype(np.float32)
        upper = matrix.astype(jnp.bfloat16)
        lower = (matrix - upper.astype(np.float32)).astype(jnp.bfloat16)
        return np.stack([upper, lower])

    return np.cos(turn).astype(np.float32), np.sin(turn).astype(np.float32), two(fore), two(back)


def correlate(lesser, greater, chunk, spot, cosine, sine, fore, back, energies):
    peers = len(lesser)
    depth, planes, lanes = greater[1].shape
    base = energies // 4
    local = planes // 2
    width = depth * lanes
    pieces = [
        piece.reshape(piece.shape[:-2] + (2, local, lanes)) for piece in (*lesser, *greater)
    ]
    shape = jax.ShapeDtypeStruct((depth, 2, local, lanes), jnp.float32)
    whole = lambda value: pl.BlockSpec(value.shape, lambda step, spot: (0,) * value.ndim)
    found = pl.pallas_call(
        functools.partial(correlate_kernel, peers, chunk),
        grid_spec=pltpu.PrefetchScalarGridSpec(
            num_scalar_prefetch=1,
            grid=(1,),
            in_specs=[whole(cosine), whole(sine), whole(fore), whole(back)] + [ANY] * (2 * peers),
            out_specs=[ANY] * peers,
            scratch_shapes=[
                pltpu.VMEM((2, depth, 2, energies, lanes), jnp.float32),
                pltpu.VMEM((RADIX, 2 * base, 2 * width), jnp.bfloat16),
                pltpu.VMEM((RADIX, 2 * base, 2 * width), jnp.bfloat16),
                pltpu.VMEM((RADIX, 2 * base, width), jnp.float32),
                pltpu.VMEM((depth, 2, energies, lanes), jnp.float32),
                pltpu.SemaphoreType.DMA((2, peers)),
                pltpu.SemaphoreType.DMA((depth, peers)),
            ],
        ),
        out_shape=[shape] * peers,
        name="correlate",
    )(spot, cosine, sine, fore, back, *pieces)
    return [piece.reshape(depth, planes, lanes) for piece in found]


def swapped(piece, hop):
    if hop == 0:
        return piece
    pairs = [(source, source ^ hop) for source in range(lax.axis_size("energy"))]
    return lax.ppermute(piece, "energy", pairs)


def exchange(pieces):
    return [swapped(piece, hop) for hop, piece in enumerate(pieces)]


def mirrored_tile(tile, side):
    return tile % side * side + tile // side


def mirror(field):
    tiles = lax.axis_size("tile")
    side = math.isqrt(tiles)
    pairs = [(tile, mirrored_tile(tile, side)) for tile in range(tiles)]
    return lax.ppermute(field, "tile", [pair for pair in pairs if pair[0] != pair[1]])


def on_device(lesser, greater):
    peers = lax.axis_size("energy")
    local, cells = greater.shape[1], greater.shape[3]
    energies = local * peers
    block = math.isqrt(cells)
    planes, rows = 2 * local, cells // LANES
    chunks = fit(rows // peers, 4)
    spot = lax.axis_index("energy").astype(jnp.int32)[None]

    tile, side = lax.axis_index("tile"), math.isqrt(lax.axis_size("tile"))
    apart = (mirrored_tile(tile, side) != tile).astype(jnp.int32)[None]

    flip = block == LANES
    if not flip:
        greater = greater.reshape(planes, block, block).swapaxes(1, 2)
    greater = greater.reshape(planes, rows, LANES)
    lesser = lesser.reshape(planes, rows, LANES)
    hops = sorted(range(peers), key=lambda hop: (-(hop.bit_count()), hop))
    early, late = hops[: peers // 2 - 1], hops[peers // 2 - 1 :]
    lesser_in = [None] * peers
    first = gather(lesser, spot, peers, early, [])
    for hop, piece in zip(early, first, strict=True):
        lesser_in[hop] = swapped(piece, hop)
    greater_out = pack(greater, spot, peers, chunks, flip, first[:1])
    second = gather(lesser, spot, peers, late, greater_out[:1])
    for hop, piece in zip(late, second, strict=True):
        lesser_in[hop] = swapped(piece, hop)

    cosine, sine, fore, back = tables(energies)
    wide = (RADIX, energies // 4, LANES)
    cosine = jnp.broadcast_to(cosine[:, :, None], wide)
    sine = jnp.broadcast_to(sine[:, :, None], wide)
    fore, back = jnp.asarray(fore), jnp.asarray(back)

    mirrored = [mirror(field) for field in greater_out]
    found, polars = [], []
    parts = 2 if chunks % 2 == 0 and rows // peers % 16 == 0 else 1
    each = chunks // parts
    result = []
    for chunk in range(chunks):
        pieces = fan(
            greater_out[chunk], mirrored[chunk], apart, [polar[0] for polar in polars[-2:-1]]
        )
        greater_in = exchange(pieces)
        polar = correlate(
            lesser_in, greater_in, chunk, spot, cosine, sine, fore, back, energies
        )
        polars.append(polar)
        found.append(exchange(polar))
        if (chunk + 1) % each == 0:
            result = [unpack(found[-each:], chunk // each, parts, spot, result)]
    return result[0].reshape(2, local, 1, cells)


def solution(mesh):
    return jax.shard_map(
        on_device,
        mesh=mesh,
        in_specs=(P(None, "energy", "tile", None), P(None, "energy", "tile", None)),
        out_specs=P(None, "energy", "tile", None),
        check_vma=False,
    )
```
